32 devices in a mesh: pipe: 4 (over y, core), ctx: 4 (over z), dp: 2 (over x).
Axes of the slice: x: 2, y: 2, z: 4, core: 2. Of those that a mesh axis runs over, the one named last changes fastest.
Arguments:
- hidden: bfloat16 [4, 1024, 4096], P('pipe', 'ctx', 'dp'), may hold values from -64 to 64
- cotangent: bfloat16 [4, 1024, 4096], P('pipe', 'ctx', 'dp'), may hold values from -6 to 6
- gain_rows: float32 [4, 4096], P('pipe', ('dp', 'ctx')), may hold values from 0.5 to 1.5
- short_taps: float32 [4, 9, 4096], P('pipe', None, ('dp', 'ctx')), may hold values from -3.5 to 3.5
- long_taps: float32 [4, 7, 4096], P('pipe', None, ('dp', 'ctx')), may hold values from -2 to 2
Outputs:
- hidden_grad: bfloat16 [4, 1024, 4096], P('pipe', 'ctx', 'dp')
- gain_grad: float32 [4, 4096], P('pipe', ('dp', 'ctx'))
- short_grad: float32 [4, 9, 4096], P('pipe', None, ('dp', 'ctx'))
- long_grad: float32 [4, 7, 4096], P('pipe', None, ('dp', 'ctx'))
The draws below stay inside these ranges and needn't reach their ends.
All inputs are finite; a program needn't handle non-finite values.
Results may differ from the reference program's by a relative error of at most 0.0056.
Values may be sent and summed in bfloat16 or wider, within the bound.
A program may use at most 64 MiB of HBM per device.

```python
import jax
import jax.numpy as jnp
from jax import lax

WIDTH = 4096
SHORT = 3
LONG = 7
SECTIONS = 4
SEQ = 1024


def draw_hidden(key, part):
    full_shape = (SECTIONS, SEQ, WIDTH)
    key_base = jax.random.fold_in(key, 11)
    key_row = jax.random.fold_in(key, 12)
    key_col = jax.random.fold_in(key, 13)
    row_scale = jnp.exp(jax.random.uniform(key_row, (SECTIONS, SEQ, 1), jnp.float32, -1.1513, 1.1513))
    base_draw = jnp.clip(jax.random.normal(key_base, full_shape, jnp.float32), -6.0, 6.0)
    col_scale = jnp.exp(jax.random.uniform(key_col, (WIDTH,), jnp.float32, -1.1513, 1.1513))
    values = base_draw * row_scale * col_scale
    return values.astype(jnp.bfloat16)


def spiked(values, own_key, source, target, shards_of, factor):
    owner, partner = [(jnp.arange(values.shape[dim]) // (values.shape[dim] // shards_of)).reshape([-1 if axis == dim else 1 for axis in range(values.ndim)]) for dim in (source, target)]
    chosen = jax.random.permutation(own_key, shards_of)[partner]
    strong = (owner == chosen) | (owner == (partner + shards_of // 2) % shards_of)
    return jnp.where(strong, factor * values, values)


def levels(stream_key, extent, cuts, smallest, largest):
    level, own = 1.0, jax.random.fold_in(stream_key, 6)
    for axis_at, parts in cuts:
        steps = jnp.exp(jax.random.uniform(jax.random.fold_in(own, axis_at), (parts,), jnp.float32, smallest / len(cuts), largest / len(cuts)))
        level = level * jnp.repeat(steps, extent[axis_at] // parts).reshape([-1 if axis == axis_at else 1 for axis in range(len(extent))])
    return level


def centred(key, shape, width, most, cuts=(), held_as=jnp.bfloat16):
    values = width * jax.random.normal(key, shape, jnp.float32)
    if cuts:
        values = values * levels(key, shape, cuts, -0.22, 0.18)
    return jnp.clip(values, -most, most).astype(held_as)


def noise_with(own_key, extent, spread, bound, cuts, heavy, held_as=jnp.bfloat16):
    result = spread * jax.random.normal(own_key, extent, jnp.float32)
    if cuts:
        result = result * levels(own_key, extent, cuts, -0.22, 0.18)
    return jnp.clip(spiked(result, jax.random.fold_in(own_key, 3), *heavy), -bound, bound).astype(held_as)


def setup_inputs(seed: int = 0) -> dict:
    keys = jax.random.split(jax.random.key(seed), 6)
    return {
        "hidden": draw_hidden(jax.random.fold_in(keys[5], 71), 0),
        "cotangent": noise_with(keys[1], (SECTIONS, SEQ, WIDTH), 1.0, 6.0, ((0, 4), (1, 4), (2, 2)), (1, 2, 4, 2.0)),
        "gain_rows": jnp.clip(1.0 + 0.1 * jax.random.normal(keys[2], (SECTIONS, WIDTH), jnp.float32), 0.5, 1.5),
        "short_taps": centred(keys[3], (SECTIONS, 3 * SHORT, WIDTH), SHORT ** -0.5, 3.5, ((0, 4), (2, 8)), jnp.float32),
        "long_taps": centred(keys[4], (SECTIONS, LONG, WIDTH), LONG ** -0.5, 2.0, ((0, 4), (2, 8)), jnp.float32),
    }


def delayed(source, places):
    if places == 0:
        return source
    zero_rows = jnp.zeros(source.shape[:-2] + (places, source.shape[-1]), source.dtype)
    return jnp.concatenate([zero_rows, source[..., :source.shape[-2] - places, :]], axis=-2)

def hyena_block(signal, gain_row, short_filter, long_filter):
    mean_square = lax.optimization_barrier(jnp.mean(signal * signal, axis=-1, keepdims=True))
    normed = signal * lax.rsqrt(mean_square + 1e-05) * gain_row
    tap_count = short_filter.shape[0] // 3
    lagged = [delayed(normed, tap_index) for tap_index in range(tap_count)]
    streams = []
    for stream_index in range(3):
        summed = short_filter[tap_count * stream_index] * lagged[0]
        for tap_index in range(1, tap_count):
            summed = summed + short_filter[tap_count * stream_index + tap_index] * lagged[tap_index]
        streams.append(summed)
    product = streams[1] * streams[2]
    mixing = long_filter[0] * product
    for tap_index in range(1, long_filter.shape[0]):
        mixing = mixing + long_filter[tap_index] * delayed(product, tap_index)
    return signal + streams[0] * mixing

def apply_block(values, filter_set):
    return hyena_block(values, filter_set[0], filter_set[1], filter_set[2])

def section_pass(packed):
    signal, cot_next, own_set, next_set = packed
    signal_f = signal.astype(jnp.float32)
    inner = apply_block(signal_f, own_set).astype(jnp.bfloat16)
    unused, pull_outer = jax.vjp(apply_block, inner.astype(jnp.float32), next_set)
    inner_grad, next_grads = pull_outer(cot_next.astype(jnp.float32))
    unused_inner, pull_inner = jax.vjp(apply_block, signal_f, own_set)
    hidden_grad, own_grads = pull_inner(inner_grad)
    return (hidden_grad.astype(jnp.bfloat16), own_grads, next_grads)

def reference(hidden, cotangent, gain_rows, short_taps, long_taps):
    cot_next = jnp.roll(cotangent, -1, axis=0)
    own_sets = (gain_rows, short_taps, long_taps)
    next_sets = (jnp.roll(gain_rows, -1, axis=0), jnp.roll(short_taps, -1, axis=0), jnp.roll(long_taps, -1, axis=0))
    hidden_grad, own_grads, next_grads = lax.map(section_pass, (hidden, cot_next, own_sets, next_sets))
    gain_grad = own_grads[0] + jnp.roll(next_grads[0], 1, axis=0)
    short_grad = own_grads[1] + jnp.roll(next_grads[1], 1, axis=0)
    long_grad = own_grads[2] + jnp.roll(next_grads[2], 1, axis=0)
    return (hidden_grad, gain_grad, short_grad, long_grad)
```

```python
import functools

import jax
import jax.numpy as jnp
from jax import lax
from jax.experimental import pallas as pl
from jax.experimental.pallas import tpu as pltpu
from jax.sharding import PartitionSpec as P

MESH = pl.DeviceIdType.MESH
F32 = jnp.float32
BF16 = jnp.bfloat16
LANES = 128
SUB = 8
EPS = 1e-05


def kernel(
    cfg,
    hid,
    cot,
    gain_in,
    short_in,
    long_in,
    out,
    gain_out,
    short_out,
    long_out,
    hbuf,
    htop,
    hbot,
    cbuf,
    cbot,
    slab,
    fr,
    filt,
    grads,
    gs,
    rg,
    xs,
    zs,
    wd,
    saved,
    parts,
    st_send,
    st_recv,
    rows,
    blank,
    loc_sem,
    halo_send,
    halo_recv,
    f_send,
    f_recv,
    g_send,
    g_recv,
    s_send,
    s_recv,
):
    npipe, nctx, ndp = cfg["npipe"], cfg["nctx"], cfg["ndp"]
    nrow, nb, cb, ntap, nshort, width = (
        cfg["nrow"], cfg["nb"], cfg["cb"], cfg["ntap"], cfg["nshort"], cfg["width"],
    )
    taps = nshort // 3
    nlong = ntap - 1 - nshort
    halo = cfg["halo"]
    total = nrow + 2 * halo
    groups = nb // SUB
    nstat = total // SUB
    pipe, ctx, dp = lax.axis_index("pipe"), lax.axis_index("ctx"), lax.axis_index("dp")
    prev = lax.rem(pipe + npipe - 1, npipe)
    follow = lax.rem(pipe + 1, npipe)

    def ctx_at(o):
        return lax.rem(ctx + o, nctx)

    def dp_at(o):
        return lax.rem(dp + o, ndp)

    def dev(p, z, d):
        return {"pipe": p, "ctx": z, "dp": d}

    def remote(src, dst, ss, rs, where):
        return pltpu.make_async_remote_copy(
            src_ref=src, dst_ref=dst, send_sem=ss, recv_sem=rs, device_id=where, device_id_type=MESH
        )

    load_hid = pltpu.make_async_copy(hid.at[0], hbuf, loc_sem.at[0])
    load_hid.start()
    blank[...] = jnp.zeros((SUB, LANES), F32)

    for k in range(ntap):
        src, row = (gain_in, 0) if k == 0 else ((short_in, k - 1) if k <= nshort else (long_in, k - 1 - nshort))
        for j in range(cb):
            cols = pl.ds(j * LANES, LANES)
            piece = src[row : row + 1, cols] if k == 0 else src[0, row : row + 1, cols]
            slab[k * cb + j : k * cb + j + 1, :] = piece
    pad = slab.shape[0] - ntap * cb
    if pad:
        slab[ntap * cb :, :] = jnp.zeros((pad, LANES), F32)
        for b in range(2):
            for z in range(nctx):
                gs[b, z, ntap * cb :, :] = jnp.zeros((pad, LANES), F32)
    fr[0, ctx] = slab[...]

    barrier = pltpu.get_barrier_semaphore()
    greeted = 0
    for p in (pipe, prev, follow):
        for o in range(nctx):
            if p is pipe and o == 0:
                continue
            pl.semaphore_signal(barrier, inc=1, device_id=dev(p, ctx_at(o), dp), device_id_type=MESH)
            greeted += 1
    for o in range(1, ndp):
        pl.semaphore_signal(barrier, inc=1, device_id=dev(pipe, ctx, dp_at(o)), device_id_type=MESH)
        greeted += 1
    pl.semaphore_wait(barrier, greeted)

    up_z = lax.max(ctx - 1, 0)
    down_z = lax.min(ctx + 1, nctx - 1)
    head, tail = pl.ds(0, halo), pl.ds(nrow - halo, halo)
    to_bot = remote(hid.at[0, head, :], hbot, halo_send.at[0], halo_recv.at[0], dev(pipe, up_z, dp))
    to_top = remote(hid.at[0, tail, :], htop, halo_send.at[1], halo_recv.at[1], dev(pipe, down_z, dp))
    to_cbot = remote(cot.at[0, head, :], cbot, halo_send.at[2], halo_recv.at[2], dev(prev, up_z, dp))
    to_cot = remote(cot.at[0], cbuf, halo_send.at[3], halo_recv.at[3], dev(prev, ctx, dp))
    has_up, has_down = ctx > 0, ctx < nctx - 1

    @pl.when(has_up)
    def _():
        to_bot.start()

    @pl.when(has_down)
    def _():
        to_top.start()

    own_sends = []
    for o in range(1, nctx):
        own_sends.append(
            remote(slab, fr.at[0, ctx], f_send.at[0, o], f_recv.at[0, ctx], dev(pipe, ctx_at(o), dp))
        )
    for o in range(nctx):
        own_sends.append(
            remote(slab, fr.at[1, ctx], f_send.at[1, o], f_recv.at[1, ctx], dev(prev, ctx_at(o), dp))
        )
    for c in own_sends:
        c.start()

    @pl.when(has_up)
    def _():
        to_cbot.start()

    to_cot.start()

    lane = lax.broadcasted_iota(jnp.int32, (SUB, LANES), 1)

    def spread(dst, first, block):
        for half in range(2):
            piece = block[half * SUB : (half + 1) * SUB, :]
            start = (first + half * SUB) * nb
            for j in range(nb):
                dst[pl.ds(start + j, SUB, stride=nb), :] = piece[:, j * LANES : (j + 1) * LANES]

    def squares(stat, first, block):
        for half in range(2):
            acc = None
            for j in range(nb):
                piece = block[half * SUB : (half + 1) * SUB, j * LANES : (j + 1) * LANES]
                acc = piece * piece if acc is None else acc + piece * piece
            value = jnp.sum(acc, axis=1, keepdims=True)
            stat = jnp.where(lane == first // SUB + half, value, stat)
        return stat

    load_hid.wait()

    def take_hidden(i, stat):
        block = hbuf[pl.ds(pl.multiple_of(i * 16, 16), 16), :].astype(F32)
        spread(xs, halo + i * 16, block)
        return squares(stat, halo + i * 16, block)

    stat = lax.fori_loop(0, nrow // 16, take_hidden, jnp.zeros((SUB, LANES), F32))

    @pl.when(has_down)
    def _():
        remote(hbot, hbot, halo_send.at[0], halo_recv.at[0], dev(pipe, down_z, dp)).wait_recv()

    @pl.when(jnp.logical_not(has_down))
    def _():
        hbot[...] = jnp.zeros(hbot.shape, BF16)

    @pl.when(has_up)
    def _():
        remote(htop, htop, halo_send.at[1], halo_recv.at[1], dev(pipe, up_z, dp)).wait_recv()

    @pl.when(jnp.logical_not(has_up))
    def _():
        htop[...] = jnp.zeros(htop.shape, BF16)

    for first, ref in ((0, htop), (halo + nrow, hbot)):
        block = ref[...].astype(F32)
        spread(xs, first, block)
        stat = squares(stat, first, block)

    def send_stat(stage, value):
        st_send[stage] = value
        st_recv[stage, dp] = value
        for o in range(1, ndp):
            remote(
                st_send.at[stage], st_recv.at[stage, dp], s_send.at[stage, o], s_recv.at[stage, dp],
                dev(pipe, ctx, dp_at(o)),
            ).start()

    def get_stat(stage):
        for o in range(1, ndp):
            there = dp_at(o)
            remote(
                st_send.at[stage], st_recv.at[stage, there], s_send.at[stage, o], s_recv.at[stage, there],
                dev(pipe, ctx, there),
            ).wait()
        value = st_recv[stage, 0]
        for d in range(1, ndp):
            value = value + st_recv[stage, d]
        return value

    def unpack(stage, value, fn):
        for i in range(nstat):
            column = jnp.sum(jnp.where(lane == i, value, 0.0), axis=1, keepdims=True)
            rows[stage, i * SUB : (i + 1) * SUB, :] = jnp.broadcast_to(fn(column), (SUB, LANES))

    def collect(lo, hi):
        def step(i, stat):
            acc = None
            for g in range(groups):
                base = (g * total + i * SUB) * SUB
                for k in range(SUB):
                    piece = parts[pl.ds(base + k, SUB, stride=SUB), :]
                    acc = piece if acc is None else acc + piece
            return jnp.where(lane == i, jnp.sum(acc, axis=1, keepdims=True), stat)

        return lax.fori_loop(lo, hi, step, jnp.zeros((SUB, LANES), F32))

    def build_filters(b):
        for z in range(nctx):
            for k in range(ntap):
                filt[b, k * nb + z * cb : k * nb + (z + 1) * cb, :] = fr[b, z, k * cb : (k + 1) * cb, :]

    def row_scale(value):
        return lax.rsqrt(value / width + EPS)

    send_stat(0, stat)
    for o in range(1, nctx):
        there = ctx_at(o)
        remote(slab, fr.at[0, there], f_send.at[0, o], f_recv.at[0, there], dev(pipe, there, dp)).wait_recv()
    build_filters(0)
    unpack(0, get_stat(0), row_scale)

    def at(w, g):
        return pl.ds(pl.multiple_of(w * nb + g * SUB, SUB), SUB)

    def row_of(stage, w):
        return jnp.broadcast_to(rows[stage, pl.ds(w, 1), :], (SUB, LANES))

    def tap(b, k, g):
        return filt[b, pl.ds(pl.multiple_of(k * nb + g * SUB, SUB), SUB), :]

    def forward(b, lo, unroll):
        def group(g, _):
            fl = [tap(b, k, g) for k in range(ntap)]
            gain, short, long = fl[0], fl[1 : 1 + nshort], fl[1 + nshort :]

            def step(it, carry):
                lag = list(carry[: taps - 1])
                past = list(carry[taps - 1 :])
                for u in range(unroll):
                    w = lo + it * unroll + u
                    x = xs[at(w, g), :]
                    xh = x * row_of(b, w)
                    seq = [xh * gain] + lag
                    streams = []
                    for j in range(3):
                        value = short[taps * j] * seq[0]
                        for i in range(1, taps):
                            value = value + short[taps * j + i] * seq[i]
                        streams.append(value)
                    products = [streams[1] * streams[2]] + past
                    mix = long[0] * products[0]
                    for i in range(1, nlong):
                        mix = mix + long[i] * products[i]
                    for n, value in enumerate((xh, streams[0], streams[1], streams[2], mix)):
                        saved[b, n, at(w, g), :] = value
                    if b == 0:
                        inner = (x + streams[0] * mix).astype(BF16).astype(F32)
                        xs[at(w, g), :] = inner
                        spot = pl.multiple_of((g * total + w) * SUB, SUB)
                        parts[pl.ds(spot, SUB), :] = inner * inner
                    lag, past = seq[:-1], products[:-1]
                return tuple(lag + past)

            zero = blank[...]
            lax.fori_loop(0, (total - lo) // unroll, step, (zero,) * (taps - 1 + nlong - 1))
            return 0

        lax.fori_loop(0, groups, group, 0)

    forward(0, 0, 8)
    send_stat(1, collect(0, nstat))

    remote(cbuf, cbuf, halo_send.at[3], halo_recv.at[3], dev(follow, ctx, dp)).wait_recv()

    @pl.when(has_down)
    def _():
        remote(cbot, cbot, halo_send.at[2], halo_recv.at[2], dev(follow, down_z, dp)).wait_recv()

    @pl.when(jnp.logical_not(has_down))
    def _():
        cbot[...] = jnp.zeros(cbot.shape, BF16)

    def take_cot(i, _):
        spread(zs, halo + i * 16, cbuf[pl.ds(pl.multiple_of(i * 16, 16), 16), :].astype(F32))
        return 0

    lax.fori_loop(0, nrow // 16, take_cot, 0)
    spread(zs, halo + nrow, cbot[...].astype(F32))
    for z in range(nctx):
        remote(slab, fr.at[1, z], f_send.at[1, z], f_recv.at[1, z], dev(follow, z, dp)).wait_recv()
    build_filters(1)
    unpack(1, get_stat(1), row_scale)
    forward(1, halo // 2, 8)

    def backward(b, top, unroll):
        def group(g, _):
            fl = [tap(b, k, g) for k in range(ntap)]
            gain, short, long = fl[0], fl[1 : 1 + nshort], fl[1 + nshort :]

            def one(w, state, acc):
                dmix_next, ds_next = state
                here = at(w, g)
                up = zs[here, :]
                if b == 0:
                    up = up + row_of(1, w) * (wd[here, :] - saved[1, 0, here, :] * row_of(2, w))
                    zs[here, :] = up
                xh, query, key, value, mix = [saved[b, n, here, :] for n in range(5)]
                dmix = [up * query] + dmix_next
                dprod = long[0] * dmix[0]
                for i in range(1, nlong):
                    dprod = dprod + long[i] * dmix[i]
                ds = [[up * mix] + ds_next[0], [dprod * value] + ds_next[1], [dprod * key] + ds_next[2]]
                dn = None
                for j in range(3):
                    for i in range(taps):
                        term = short[taps * j + i] * ds[j][i]
                        dn = term if dn is None else dn + term
                weighted = gain * dn
                wd[here, :] = weighted
                spot = pl.multiple_of((g * total + w) * SUB, SUB)
                parts[pl.ds(spot, SUB), :] = xh * weighted
                if acc is not None:
                    product, normed = key * value, xh * gain
                    fresh = [acc[0] + xh * dn]
                    for j in range(3):
                        for i in range(taps):
                            fresh.append(acc[1 + taps * j + i] + normed * ds[j][i])
                    for i in range(nlong):
                        fresh.append(acc[1 + nshort + i] + product * dmix[i])
                    acc = fresh
                return (dmix[:-1], [d[:-1] for d in ds]), acc

            def flat(state):
                return tuple(state[0]) + tuple(v for d in state[1] for v in d)

            def unflat(vals):
                n = nlong - 1
                rest = vals[n:]
                m = taps - 1
                return list(vals[:n]), [list(rest[j * m : (j + 1) * m]) for j in range(3)]

            nstate = nlong - 1 + 3 * (taps - 1)

            def warm(it, carry):
                state = unflat(carry)
                for u in range(unroll):
                    state, _ = one(top - 1 - it * unroll - u, state, None)
                return flat(state)

            def main(it, carry):
                state, acc = unflat(carry[:nstate]), list(carry[nstate:])
                for u in range(unroll):
                    state, acc = one(halo + nrow - 1 - it * unroll - u, state, acc)
                return flat(state) + tuple(acc)

            zero = blank[...]
            carry = lax.fori_loop(0, (top - halo - nrow) // unroll, warm, (zero,) * nstate)
            carry = lax.fori_loop(0, nrow // unroll, main, carry + (zero,) * ntap)
            for k in range(ntap):
                grads[pl.ds(pl.multiple_of(k * nb + g * SUB, SUB), SUB), :] = carry[nstate + k]
            return 0

        lax.fori_loop(0, groups, group, 0)

    def split_grads(b):
        for z in range(nctx):
            for k in range(ntap):
                gs[b, z, k * cb : (k + 1) * cb, :] = grads[k * nb + z * cb : k * nb + (z + 1) * cb, :]

    def mean_of(value):
        return value / width

    backward(1, total, 4)
    send_stat(2, collect(halo // SUB, nstat))
    split_grads(1)
    grad_sends = []
    for o in range(nctx):
        z = ctx_at(o)
        grad_sends.append(
            remote(gs.at[1, z], rg.at[1, ctx], g_send.at[1, o], g_recv.at[1, ctx], dev(follow, z, dp))
        )
        grad_sends[-1].start()
    unpack(2, get_stat(2), mean_of)

    backward(0, halo + nrow + halo // 2, 4)
    send_stat(3, collect(halo // SUB, (halo + nrow) // SUB))
    split_grads(0)
    for o in range(1, nctx):
        z = ctx_at(o)
        grad_sends.append(
            remote(gs.at[0, z], rg.at[0, ctx], g_send.at[0, o], g_recv.at[0, ctx], dev(pipe, z, dp))
        )
        grad_sends[-1].start()
    rg[0, ctx] = gs[0, ctx]
    unpack(3, get_stat(3), mean_of)

    def finish(i, _):
        w = halo + i * 16
        halves = [pl.multiple_of(w + half * SUB, SUB) for half in range(2)]
        scales = [rows[0, pl.ds(h, SUB), :] for h in halves]
        means = [rows[3, pl.ds(h, SUB), :] for h in halves]
        for j in range(nb):
            pieces = []
            for half in range(2):
                here = pl.ds(halves[half] * nb + j, SUB, stride=nb)
                pieces.append(zs[here, :] + scales[half] * (wd[here, :] - saved[0, 0, here, :] * means[half]))
            out[0, pl.ds(pl.multiple_of(i * 16, 16), 16), j * LANES : (j + 1) * LANES] = jnp.concatenate(
                pieces, axis=0
            ).astype(BF16)
        return 0

    lax.fori_loop(0, nrow // 16, finish, 0)

    for z in range(nctx):
        remote(gs.at[1, z], rg.at[1, z], g_send.at[1, z], g_recv.at[1, z], dev(prev, z, dp)).wait_recv()
    for o in range(1, nctx):
        z = ctx_at(o)
        remote(gs.at[0, z], rg.at[0, z], g_send.at[0, o], g_recv.at[0, z], dev(pipe, z, dp)).wait_recv()
    result = rg[0, 0] + rg[1, 0]
    for z in range(1, nctx):
        result = result + (rg[0, z] + rg[1, z])
    for k in range(ntap):
        for j in range(cb):
            cols = pl.ds(j * LANES, LANES)
            piece = result[k * cb + j : k * cb + j + 1, :]
            if k == 0:
                gain_out[0:1, cols] = piece
            elif k <= nshort:
                short_out[0, k - 1 : k, cols] = piece
            else:
                long_out[0, k - 1 - nshort : k - nshort, cols] = piece

    @pl.when(has_up)
    def _():
        to_bot.wait_send()
        to_cbot.wait_send()

    @pl.when(has_down)
    def _():
        to_top.wait_send()

    to_cot.wait_send()
    for c in own_sends + grad_sends:
        c.wait_send()


def per_device(mesh, hidden, cotangent, gain_rows, short_taps, long_taps):
    npipe, nctx, ndp = mesh.shape["pipe"], mesh.shape["ctx"], mesh.shape["dp"]
    nrow, chans = hidden.shape[1], hidden.shape[2]
    own = gain_rows.shape[1]
    wide = -(-own // LANES) * LANES
    nshort, nlong = short_taps.shape[1], long_taps.shape[1]
    ntap = 1 + nshort + nlong
    cb = wide // LANES
    nb = nctx * cb
    halo = 2 * (nshort // 3 + nlong - 2)
    total = nrow + 2 * halo
    slab_rows = -(-ntap * cb // SUB) * SUB

    def widen(values):
        if wide == own:
            return values
        lead = values.shape[:-1]
        blocks = values.reshape(lead + (-1, own))
        blocks = jnp.pad(blocks, [(0, 0)] * (len(lead) + 1) + [(0, wide - own)])
        return blocks.reshape(lead + (-1,))

    def narrow(values):
        if wide == own:
            return values
        lead = values.shape[:-1]
        return values.reshape(lead + (-1, wide))[..., :own].reshape(lead + (-1,))

    cfg = dict(
        npipe=npipe, nctx=nctx, ndp=ndp, nrow=nrow, nb=nb, cb=cb, ntap=ntap, nshort=nshort,
        width=float(chans * ndp), halo=halo,
    )
    full = nb * LANES
    dma = pltpu.SemaphoreType.DMA
    vmem = pl.BlockSpec(memory_space=pltpu.VMEM)
    anywhere = pl.BlockSpec(memory_space=pl.ANY)
    outs = pl.pallas_call(
        functools.partial(kernel, cfg),
        out_shape=(
            jax.ShapeDtypeStruct((1, nrow, full), BF16),
            jax.ShapeDtypeStruct((1, wide), F32),
            jax.ShapeDtypeStruct((1, nshort, wide), F32),
            jax.ShapeDtypeStruct((1, nlong, wide), F32),
        ),
        in_specs=[anywhere, anywhere, vmem, vmem, vmem],
        out_specs=(vmem, vmem, vmem, vmem),
        scratch_shapes=[
            pltpu.VMEM((nrow, full), BF16),
            pltpu.VMEM((halo, full), BF16),
            pltpu.VMEM((halo, full), BF16),
            pltpu.VMEM((nrow, full), BF16),
            pltpu.VMEM((halo, full), BF16),
            pltpu.VMEM((slab_rows, LANES), F32),
            pltpu.VMEM((2, nctx, slab_rows, LANES), F32),
            pltpu.VMEM((2, ntap * nb, LANES), F32),
            pltpu.VMEM((ntap * nb, LANES), F32),
            pltpu.VMEM((2, nctx, slab_rows, LANES), F32),
            pltpu.VMEM((2, nctx, slab_rows, LANES), F32),
            pltpu.VMEM((total * nb, LANES), F32),
            pltpu.VMEM((total * nb, LANES), F32),
            pltpu.VMEM((total * nb, LANES), F32),
            pltpu.VMEM((2, 5, total * nb, LANES), F32),
            pltpu.VMEM((total * nb, LANES), F32),
            pltpu.VMEM((4, SUB, LANES), F32),
            pltpu.VMEM((4, ndp, SUB, LANES), F32),
            pltpu.VMEM((4, total, LANES), F32),
            pltpu.VMEM((SUB, LANES), F32),
            dma((1,)),
            dma((4,)),
            dma((4,)),
            dma((2, nctx)),
            dma((2, nctx)),
            dma((2, nctx)),
            dma((2, nctx)),
            dma((4, ndp)),
            dma((4, ndp)),
        ],
        compiler_params=pltpu.CompilerParams(
            collective_id=0, has_side_effects=True, vmem_limit_bytes=56 * 1024 * 1024
        ),
        name="relay",
    )(widen(hidden), widen(cotangent), widen(gain_rows), widen(short_taps), widen(long_taps))
    return tuple(narrow(o) for o in outs)


def solution(mesh):
    in_specs = (
        P("pipe", "ctx", "dp"),
        P("pipe", "ctx", "dp"),
        P("pipe", ("dp", "ctx")),
        P("pipe", None, ("dp", "ctx")),
        P("pipe", None, ("dp", "ctx")),
    )
    out_specs = (
        P("pipe", "ctx", "dp"),
        P("pipe", ("dp", "ctx")),
        P("pipe", None, ("dp", "ctx")),
        P("pipe", None, ("dp", "ctx")),
    )
    return jax.shard_map(
        functools.partial(per_device, mesh), mesh=mesh, in_specs=in_specs, out_specs=out_specs, check_vma=False
    )
```

```python
import functools

import jax
import jax.numpy as jnp
from jax import lax
from jax.experimental import pallas as pl
from jax.experimental.pallas import tpu as pltpu
from jax.sharding import PartitionSpec as P

MESH = pl.DeviceIdType.MESH
F32 = jnp.float32
BF16 = jnp.bfloat16
LANES = 128
SUB = 8
EPS = 1e-05


def kernel(
    cfg,
    hid,
    cot,
    gain_in,
    short_in,
    long_in,
    out,
    gain_out,
    short_out,
    long_out,
    hbuf,
    htop,
    hbot,
    cbuf,
    cbot,
    slab,
    fr,
    filt,
    grads,
    gs,
    rg,
    xs,
    ys,
    zs,
    wd_outer,
    wd_inner,
    saved,
    parts,
    st_send,
    st_recv,
    rows,
    blank,
    loc_sem,
    halo_send,
    halo_recv,
    f_send,
    f_recv,
    g_send,
    g_recv,
    s_send,
    s_recv,
):
    npipe, nctx, ndp = cfg["npipe"], cfg["nctx"], cfg["ndp"]
    nrow, nb, cb, ntap, nshort, width = (
        cfg["nrow"], cfg["nb"], cfg["cb"], cfg["ntap"], cfg["nshort"], cfg["width"],
    )
    taps = nshort // 3
    nlong = ntap - 1 - nshort
    halo = cfg["halo"]
    total = nrow + 2 * halo
    groups = nb // SUB
    nstat = total // SUB
    pipe, ctx, dp = lax.axis_index("pipe"), lax.axis_index("ctx"), lax.axis_index("dp")
    prev = lax.rem(pipe + npipe - 1, npipe)
    follow = lax.rem(pipe + 1, npipe)

    def ctx_at(o):
        return lax.rem(ctx + o, nctx)

    def dp_at(o):
        return lax.rem(dp + o, ndp)

    def dev(p, z, d):
        return {"pipe": p, "ctx": z, "dp": d}

    def remote(src, dst, ss, rs, where):
        return pltpu.make_async_remote_copy(
            src_ref=src, dst_ref=dst, send_sem=ss, recv_sem=rs, device_id=where, device_id_type=MESH
        )

    load_hid = pltpu.make_async_copy(hid.at[0], hbuf, loc_sem.at[0])
    load_hid.start()
    blank[...] = jnp.zeros((SUB, LANES), F32)

    for k in range(ntap):
        src, row = (gain_in, 0) if k == 0 else ((short_in, k - 1) if k <= nshort else (long_in, k - 1 - nshort))
        for j in range(cb):
            cols = pl.ds(j * LANES, LANES)
            piece = src[row : row + 1, cols] if k == 0 else src[row, 0:1, cols]
            slab[k * cb + j : k * cb + j + 1, :] = piece
    pad = slab.shape[0] - ntap * cb
    if pad:
        slab[ntap * cb :, :] = jnp.zeros((pad, LANES), F32)
        for b in range(2):
            for z in range(nctx):
                gs[b, z, ntap * cb :, :] = jnp.zeros((pad, LANES), F32)
    fr[0, ctx] = slab[...]

    barrier = pltpu.get_barrier_semaphore()
    greeted = 0
    for p in (pipe, prev, follow):
        for o in range(nctx):
            if p is pipe and o == 0:
                continue
            pl.semaphore_signal(barrier, inc=1, device_id=dev(p, ctx_at(o), dp), device_id_type=MESH)
            greeted += 1
    for o in range(1, ndp):
        pl.semaphore_signal(barrier, inc=1, device_id=dev(pipe, ctx, dp_at(o)), device_id_type=MESH)
        greeted += 1
    pl.semaphore_wait(barrier, greeted)

    up_z = lax.max(ctx - 1, 0)
    down_z = lax.min(ctx + 1, nctx - 1)
    head, tail = pl.ds(0, halo), pl.ds(nrow - halo, halo)
    to_bot = remote(hid.at[0, head, :], hbot, halo_send.at[0], halo_recv.at[0], dev(pipe, up_z, dp))
    to_top = remote(hid.at[0, tail, :], htop, halo_send.at[1], halo_recv.at[1], dev(pipe, down_z, dp))
    to_cbot = remote(cot.at[0, head, :], cbot, halo_send.at[2], halo_recv.at[2], dev(prev, up_z, dp))
    to_cot = remote(cot.at[0], cbuf, halo_send.at[3], halo_recv.at[3], dev(prev, ctx, dp))
    has_up, has_down = ctx > 0, ctx < nctx - 1

    @pl.when(has_up)
    def _():
        to_bot.start()

    @pl.when(has_down)
    def _():
        to_top.start()

    own_sends = []
    for o in range(1, nctx):
        own_sends.append(
            remote(slab, fr.at[0, ctx], f_send.at[0, o], f_recv.at[0, ctx], dev(pipe, ctx_at(o), dp))
        )
    for o in range(nctx):
        own_sends.append(
            remote(slab, fr.at[1, ctx], f_send.at[1, o], f_recv.at[1, ctx], dev(prev, ctx_at(o), dp))
        )
    for c in own_sends:
        c.start()

    @pl.when(has_up)
    def _():
        to_cbot.start()

    to_cot.start()

    lane = lax.broadcasted_iota(jnp.int32, (SUB, LANES), 1)

    def spread(dst, first, block):
        for half in range(2):
            piece = block[half * SUB : (half + 1) * SUB, :]
            start = (first + half * SUB) * nb
            for j in range(nb):
                dst[pl.ds(start + j, SUB, stride=nb), :] = piece[:, j * LANES : (j + 1) * LANES]

    def squares(stat, first, block):
        for half in range(2):
            acc = None
            for j in range(nb):
                piece = block[half * SUB : (half + 1) * SUB, j * LANES : (j + 1) * LANES]
                acc = piece * piece if acc is None else acc + piece * piece
            value = jnp.sum(acc, axis=1, keepdims=True)
            stat = jnp.where(lane == first // SUB + half, value, stat)
        return stat

    load_hid.wait()

    def take_hidden(i, stat):
        block = hbuf[pl.ds(pl.multiple_of(i * 16, 16), 16), :].astype(F32)
        spread(xs, halo + i * 16, block)
        return squares(stat, halo + i * 16, block)

    stat = lax.fori_loop(0, nrow // 16, take_hidden, jnp.zeros((SUB, LANES), F32))

    @pl.when(has_down)
    def _():
        remote(hbot, hbot, halo_send.at[0], halo_recv.at[0], dev(pipe, down_z, dp)).wait_recv()

    @pl.when(jnp.logical_not(has_down))
    def _():
        hbot[...] = jnp.zeros(hbot.shape, BF16)

    @pl.when(has_up)
    def _():
        remote(htop, htop, halo_send.at[1], halo_recv.at[1], dev(pipe, up_z, dp)).wait_recv()

    @pl.when(jnp.logical_not(has_up))
    def _():
        htop[...] = jnp.zeros(htop.shape, BF16)

    for first, ref in ((0, htop), (halo + nrow, hbot)):
        block = ref[...].astype(F32)
        spread(xs, first, block)
        stat = squares(stat, first, block)

    def send_stat(stage, value):
        st_send[stage] = value
        st_recv[stage, dp] = value
        for o in range(1, ndp):
            remote(
                st_send.at[stage], st_recv.at[stage, dp], s_send.at[stage, o], s_recv.at[stage, dp],
                dev(pipe, ctx, dp_at(o)),
            ).start()

    def get_stat(stage):
        for o in range(1, ndp):
            there = dp_at(o)
            remote(
                st_send.at[stage], st_recv.at[stage, there], s_send.at[stage, o], s_recv.at[stage, there],
                dev(pipe, ctx, there),
            ).wait()
        value = st_recv[stage, 0]
        for d in range(1, ndp):
            value = value + st_recv[stage, d]
        return value

    def unpack(stage, value, fn):
        for i in range(nstat):
            column = jnp.sum(jnp.where(lane == i, value, 0.0), axis=1, keepdims=True)
            rows[stage, i * SUB : (i + 1) * SUB, :] = jnp.broadcast_to(fn(column), (SUB, LANES))

    def collect(lo, hi):
        def step(i, stat):
            acc = None
            for g in range(groups):
                base = (g * total + i * SUB) * SUB
                for k in range(SUB):
                    piece = parts[pl.ds(base + k, SUB, stride=SUB), :]
                    acc = piece if acc is None else acc + piece
            return jnp.where(lane == i, jnp.sum(acc, axis=1, keepdims=True), stat)

        return lax.fori_loop(lo, hi, step, jnp.zeros((SUB, LANES), F32), unroll=6)

    def build_filters(b):
        for z in range(nctx):
            for k in range(ntap):
                filt[b, k * nb + z * cb : k * nb + (z + 1) * cb, :] = fr[b, z, k * cb : (k + 1) * cb, :]

    def row_scale(value):
        return lax.rsqrt(value / width + EPS)

    send_stat(0, stat)
    for o in range(1, nctx):
        there = ctx_at(o)
        remote(slab, fr.at[0, there], f_send.at[0, o], f_recv.at[0, there], dev(pipe, there, dp)).wait_recv()
    build_filters(0)
    unpack(0, get_stat(0), row_scale)

    def at(w, g):
        return pl.ds(pl.multiple_of(w * nb + g * SUB, SUB), SUB)

    def row_of(stage, w):
        return jnp.broadcast_to(rows[stage, pl.ds(w, 1), :], (SUB, LANES))

    def tap(b, k, g):
        return filt[b, pl.ds(pl.multiple_of(k * nb + g * SUB, SUB), SUB), :]

    def forward(b, lo, unroll):
        def group(g, _):
            fl = [tap(b, k, g) for k in range(ntap)]
            gain, short, long = fl[0], fl[1 : 1 + nshort], fl[1 + nshort :]

            def step(it, carry):
                lag = list(carry[: taps - 1])
                past = list(carry[taps - 1 :])
                for u in range(unroll):
                    w = lo + it * unroll + u
                    x = (xs if b == 0 else ys)[at(w, g), :]
                    xh = x * row_of(b, w)
                    seq = [xh * gain] + lag
                    streams = []
                    for j in range(3):
                        value = short[taps * j] * seq[0]
                        for i in range(1, taps):
                            value = value + short[taps * j + i] * seq[i]
                        streams.append(value)
                    products = [streams[1] * streams[2]] + past
                    mix = long[0] * products[0]
                    for i in range(1, nlong):
                        mix = mix + long[i] * products[i]
                    for n, value in enumerate((xh, streams[0], streams[1], streams[2], mix)):
                        saved[b, n, at(w, g), :] = value
                    if b == 0:
                        inner = (x + streams[0] * mix).astype(BF16).astype(F32)
                        ys[at(w, g), :] = inner
                        spot = pl.multiple_of((g * total + w) * SUB, SUB)
                        parts[pl.ds(spot, SUB), :] = inner * inner
                    lag, past = seq[:-1], products[:-1]
                return tuple(lag + past)

            zero = blank[...]
            lax.fori_loop(0, (total - lo) // unroll, step, (zero,) * (taps - 1 + nlong - 1))
            return 0

        lax.fori_loop(0, groups, group, 0)

    forward(0, 0, 8)
    send_stat(1, collect(0, nstat))

    for z in range(nctx):
        remote(slab, fr.at[1, z], f_send.at[1, z], f_recv.at[1, z], dev(follow, z, dp)).wait_recv()
    build_filters(1)
    unpack(1, get_stat(1), row_scale)
    forward(1, halo // 2, 8)

    remote(cbuf, cbuf, halo_send.at[3], halo_recv.at[3], dev(follow, ctx, dp)).wait_recv()

    @pl.when(has_down)
    def _():
        remote(cbot, cbot, halo_send.at[2], halo_recv.at[2], dev(follow, down_z, dp)).wait_recv()

    @pl.when(jnp.logical_not(has_down))
    def _():
        cbot[...] = jnp.zeros(cbot.shape, BF16)

    def take_cot(i, _):
        spread(zs, halo + i * 16, cbuf[pl.ds(pl.multiple_of(i * 16, 16), 16), :].astype(F32))
        return 0

    lax.fori_loop(0, nrow // 16, take_cot, 0)
    spread(zs, halo + nrow, cbot[...].astype(F32))

    def backward(b, top, unroll):
        def group(g, _):
            fl = [tap(b, k, g) for k in range(ntap)]
            gain, short, long = fl[0], fl[1 : 1 + nshort], fl[1 + nshort :]

            def one(w, state, acc):
                dmix_next, ds_next = state
                here = at(w, g)
                up = zs[here, :]
                if b == 0:
                    up = up + row_of(1, w) * (wd_outer[here, :] - saved[1, 0, here, :] * row_of(2, w))
                    xs[here, :] = up
                xh, query, key, value, mix = [saved[b, n, here, :] for n in range(5)]
                dmix = [up * query] + dmix_next
                dprod = long[0] * dmix[0]
                for i in range(1, nlong):
                    dprod = dprod + long[i] * dmix[i]
                ds = [[up * mix] + ds_next[0], [dprod * value] + ds_next[1], [dprod * key] + ds_next[2]]
                dn = None
                for j in range(3):
                    for i in range(taps):
                        term = short[taps * j + i] * ds[j][i]
                        dn = term if dn is None else dn + term
                weighted = gain * dn
                (wd_outer if b == 1 else wd_inner)[here, :] = weighted
                spot = pl.multiple_of((g * total + w) * SUB, SUB)
                parts[pl.ds(spot, SUB), :] = xh * weighted
                if acc is not None:
                    product, normed = key * value, xh * gain
                    fresh = [acc[0] + xh * dn]
                    for j in range(3):
                        for i in range(taps):
                            fresh.append(acc[1 + taps * j + i] + normed * ds[j][i])
                    for i in range(nlong):
                        fresh.append(acc[1 + nshort + i] + product * dmix[i])
                    acc = fresh
                return (dmix[:-1], [d[:-1] for d in ds]), acc

            def flat(state):
                return tuple(state[0]) + tuple(v for d in state[1] for v in d)

            def unflat(vals):
                n = nlong - 1
                rest = vals[n:]
                m = taps - 1
                return list(vals[:n]), [list(rest[j * m : (j + 1) * m]) for j in range(3)]

            nstate = nlong - 1 + 3 * (taps - 1)

            def warm(it, carry):
                state = unflat(carry)
                for u in range(unroll):
                    state, _ = one(top - 1 - it * unroll - u, state, None)
                return flat(state)

            def main(it, carry):
                state, acc = unflat(carry[:nstate]), list(carry[nstate:])
                for u in range(unroll):
                    state, acc = one(halo + nrow - 1 - it * unroll - u, state, acc)
                return flat(state) + tuple(acc)

            zero = blank[...]
            carry = lax.fori_loop(0, (top - halo - nrow) // unroll, warm, (zero,) * nstate)
            carry = lax.fori_loop(0, nrow // unroll, main, carry + (zero,) * ntap)
            for k in range(ntap):
                grads[pl.ds(pl.multiple_of(k * nb + g * SUB, SUB), SUB), :] = carry[nstate + k]
            return 0

        lax.fori_loop(0, groups, group, 0)

    def split_grads(b):
        for z in range(nctx):
            for k in range(ntap):
                gs[b, z, k * cb : (k + 1) * cb, :] = grads[k * nb + z * cb : k * nb + (z + 1) * cb, :]

    def mean_of(value):
        return value / width

    backward(1, total, 4)
    send_stat(2, collect(halo // SUB, nstat))
    split_grads(1)
    grad_sends = []
    for o in range(nctx):
        z = ctx_at(o)
        grad_sends.append(
            remote(gs.at[1, z], rg.at[1, ctx], g_send.at[1, o], g_recv.at[1, ctx], dev(follow, z, dp))
        )
        grad_sends[-1].start()
    unpack(2, get_stat(2), mean_of)

    backward(0, halo + nrow + halo // 2, 4)
    send_stat(3, collect(halo // SUB, (halo + nrow) // SUB))
    split_grads(0)
    for o in range(1, nctx):
        z = ctx_at(o)
        grad_sends.append(
            remote(gs.at[0, z], rg.at[0, ctx], g_send.at[0, o], g_recv.at[0, ctx], dev(pipe, z, dp))
        )
        grad_sends[-1].start()
    rg[0, ctx] = gs[0, ctx]
    unpack(3, get_stat(3), mean_of)

    def finish(i, _):
        w = halo + i * 16
        halves = [pl.multiple_of(w + half * SUB, SUB) for half in range(2)]
        scales = [rows[0, pl.ds(h, SUB), :] for h in halves]
        means = [rows[3, pl.ds(h, SUB), :] for h in halves]
        for j in range(nb):
            pieces = []
            for half in range(2):
                here = pl.ds(halves[half] * nb + j, SUB, stride=nb)
                pieces.append(xs[here, :] + scales[half] * (wd_inner[here, :] - saved[0, 0, here, :] * means[half]))
            out[0, pl.ds(pl.multiple_of(i * 16, 16), 16), j * LANES : (j + 1) * LANES] = jnp.concatenate(
                pieces, axis=0
            ).astype(BF16)
        return 0

    lax.fori_loop(0, nrow // 16, finish, 0)

    for z in range(nctx):
        remote(gs.at[1, z], rg.at[1, z], g_send.at[1, z], g_recv.at[1, z], dev(prev, z, dp)).wait_recv()
    for o in range(1, nctx):
        z = ctx_at(o)
        remote(gs.at[0, z], rg.at[0, z], g_send.at[0, o], g_recv.at[0, z], dev(pipe, z, dp)).wait_recv()
    result = rg[0, 0] + rg[1, 0]
    for z in range(1, nctx):
        result = result + (rg[0, z] + rg[1, z])
    for k in range(ntap):
        for j in range(cb):
            cols = pl.ds(j * LANES, LANES)
            piece = result[k * cb + j : k * cb + j + 1, :]
            if k == 0:
                gain_out[0:1, cols] = piece
            elif k <= nshort:
                short_out[k - 1, 0:1, cols] = piece
            else:
                long_out[k - 1 - nshort, 0:1, cols] = piece

    @pl.when(has_up)
    def _():
        to_bot.wait_send()
        to_cbot.wait_send()

    @pl.when(has_down)
    def _():
        to_top.wait_send()

    to_cot.wait_send()
    for c in own_sends + grad_sends:
        c.wait_send()


def handed_on(a0, a1, a2, a3, b0, b1, b2, b3):
    b0[...] = a0[...]

    @pl.when(pl.program_id(0) == 0)
    def _():
        b1[...] = a1[...]
        b2[...] = a2[...]
        b3[...] = a3[...]


def swap(values):
    return jnp.transpose(values, (1, 0, 2))


def per_device(mesh, hidden, cotangent, gain_rows, short_taps, long_taps):
    npipe, nctx, ndp = mesh.shape["pipe"], mesh.shape["ctx"], mesh.shape["dp"]
    nrow, chans = hidden.shape[1], hidden.shape[2]
    own = gain_rows.shape[1]
    wide = -(-own // LANES) * LANES
    nshort, nlong = short_taps.shape[1], long_taps.shape[1]
    ntap = 1 + nshort + nlong
    cb = wide // LANES
    nb = nctx * cb
    halo = 2 * (nshort // 3 + nlong - 2)
    total = nrow + 2 * halo
    slab_rows = -(-ntap * cb // SUB) * SUB

    def widen(values):
        if wide == own:
            return values
        lead = values.shape[:-1]
        blocks = values.reshape(lead + (-1, own))
        blocks = jnp.pad(blocks, [(0, 0)] * (len(lead) + 1) + [(0, wide - own)])
        return blocks.reshape(lead + (-1,))

    def narrow(values):
        if wide == own:
            return values
        lead = values.shape[:-1]
        return values.reshape(lead + (-1, wide))[..., :own].reshape(lead + (-1,))

    cfg = dict(
        npipe=npipe, nctx=nctx, ndp=ndp, nrow=nrow, nb=nb, cb=cb, ntap=ntap, nshort=nshort,
        width=float(chans * ndp), halo=halo,
    )
    full = nb * LANES
    dma = pltpu.SemaphoreType.DMA
    vmem = pl.BlockSpec(memory_space=pltpu.VMEM)
    anywhere = pl.BlockSpec(memory_space=pl.ANY)
    shapes = (
        jax.ShapeDtypeStruct((1, nrow, full), BF16),
        jax.ShapeDtypeStruct((1, wide), F32),
        jax.ShapeDtypeStruct((nshort, 1, wide), F32),
        jax.ShapeDtypeStruct((nlong, 1, wide), F32),
    )
    outs = pl.pallas_call(
        functools.partial(kernel, cfg),
        out_shape=shapes,
        in_specs=[anywhere, anywhere, vmem, vmem, vmem],
        out_specs=(vmem, vmem, vmem, vmem),
        scratch_shapes=[
            pltpu.VMEM((nrow, full), BF16),
            pltpu.VMEM((halo, full), BF16),
            pltpu.VMEM((halo, full), BF16),
            pltpu.VMEM((nrow, full), BF16),
            pltpu.VMEM((halo, full), BF16),
            pltpu.VMEM((slab_rows, LANES), F32),
            pltpu.VMEM((2, nctx, slab_rows, LANES), F32),
            pltpu.VMEM((2, ntap * nb, LANES), F32),
            pltpu.VMEM((ntap * nb, LANES), F32),
            pltpu.VMEM((2, nctx, slab_rows, LANES), F32),
            pltpu.VMEM((2, nctx, slab_rows, LANES), F32),
            pltpu.VMEM((total * nb, LANES), F32),
            pltpu.VMEM((total * nb, LANES), F32),
            pltpu.VMEM((total * nb, LANES), F32),
            pltpu.VMEM((total * nb, LANES), F32),
            pltpu.VMEM((total * nb, LANES), F32),
            pltpu.VMEM((2, 5, total * nb, LANES), F32),
            pltpu.VMEM((total * nb, LANES), F32),
            pltpu.VMEM((4, SUB, LANES), F32),
            pltpu.VMEM((4, ndp, SUB, LANES), F32),
            pltpu.VMEM((4, total, LANES), F32),
            pltpu.VMEM((SUB, LANES), F32),
            dma((1,)),
            dma((4,)),
            dma((4,)),
            dma((2, nctx)),
            dma((2, nctx)),
            dma((2, nctx)),
            dma((2, nctx)),
            dma((4, ndp)),
            dma((4, ndp)),
        ],
        compiler_params=pltpu.CompilerParams(
            collective_id=0, has_side_effects=True, vmem_limit_bytes=56 * 1024 * 1024
        ),
        name="relay",
    )(widen(hidden), widen(cotangent), widen(gain_rows), swap(widen(short_taps)), swap(widen(long_taps)))
    passed = [pl.BlockSpec((1, nrow // 4, full), lambda i: (0, i, 0))] + [
        pl.BlockSpec(o.shape, functools.partial(lambda rank, i: (0,) * rank, len(o.shape))) for o in shapes[1:]
    ]
    outs = pl.pallas_call(
        handed_on,
        out_shape=shapes,
        grid=(4,),
        in_specs=passed,
        out_specs=tuple(passed),
        name="handed_on",
    )(*outs)
    return tuple(narrow(o) for o in (outs[0], outs[1], swap(outs[2]), swap(outs[3])))


def solution(mesh):
    in_specs = (
        P("pipe", "ctx", "dp"),
        P("pipe", "ctx", "dp"),
        P("pipe", ("dp", "ctx")),
        P("pipe", None, ("dp", "ctx")),
        P("pipe", None, ("dp", "ctx")),
    )
    out_specs = (
        P("pipe", "ctx", "dp"),
        P("pipe", ("dp", "ctx")),
        P("pipe", None, ("dp", "ctx")),
        P("pipe", None, ("dp", "ctx")),
    )
    return jax.shard_map(
        functools.partial(per_device, mesh), mesh=mesh, in_specs=in_specs, out_specs=out_specs, check_vma=False
    )
```

```python
import functools

import jax
import jax.numpy as jnp
from jax import lax
from jax.experimental import pallas as pl
from jax.experimental.pallas import tpu as pltpu
from jax.sharding import PartitionSpec as P

MESH = pl.DeviceIdType.MESH
F32 = jnp.float32
BF16 = jnp.bfloat16
LANES = 128
SUB = 8
EPS = 1e-05


def kernel(
    cfg,
    hid,
    cot,
    gain_in,
    short_in,
    long_in,
    out,
    gain_out,
    short_out,
    long_out,
    hbuf,
    htop,
    hbot,
    cbuf,
    cbot,
    slab,
    fr,
    filt,
    grads,
    gs,
    rg,
    xs,
    ys,
    zs,
    wd_outer,
    wd_inner,
    saved,
    parts,
    st_send,
    st_recv,
    rows,
    blank,
    loc_sem,
    halo_send,
    halo_recv,
    f_send,
    f_recv,
    g_send,
    g_recv,
    s_send,
    s_recv,
):
    npipe, nctx, ndp = cfg["npipe"], cfg["nctx"], cfg["ndp"]
    nrow, nb, cb, ntap, nshort, width = (
        cfg["nrow"], cfg["nb"], cfg["cb"], cfg["ntap"], cfg["nshort"], cfg["width"],
    )
    taps = nshort // 3
    nlong = ntap - 1 - nshort
    halo = cfg["halo"]
    total = nrow + 2 * halo
    groups = nb // SUB
    nstat = total // SUB
    pipe, ctx, dp = lax.axis_index("pipe"), lax.axis_index("ctx"), lax.axis_index("dp")
    prev = lax.rem(pipe + npipe - 1, npipe)
    follow = lax.rem(pipe + 1, npipe)

    def ctx_at(o):
        return lax.rem(ctx + o, nctx)

    def dp_at(o):
        return lax.rem(dp + o, ndp)

    def dev(p, z, d):
        return {"pipe": p, "ctx": z, "dp": d}

    def remote(src, dst, ss, rs, where):
        return pltpu.make_async_remote_copy(
            src_ref=src, dst_ref=dst, send_sem=ss, recv_sem=rs, device_id=where, device_id_type=MESH
        )

    load_hid = pltpu.make_async_copy(hid.at[0], hbuf, loc_sem.at[0])
    load_hid.start()
    blank[...] = jnp.zeros((SUB, LANES), F32)

    for k in range(ntap):
        src, row = (gain_in, 0) if k == 0 else ((short_in, k - 1) if k <= nshort else (long_in, k - 1 - nshort))
        for j in range(cb):
            cols = pl.ds(j * LANES, LANES)
            piece = src[row : row + 1, cols] if k == 0 else src[row, 0:1, cols]
            slab[k * cb + j : k * cb + j + 1, :] = piece
    pad = slab.shape[0] - ntap * cb
    if pad:
        slab[ntap * cb :, :] = jnp.zeros((pad, LANES), F32)
        for b in range(2):
            for z in range(nctx):
                gs[b, z, ntap * cb :, :] = jnp.zeros((pad, LANES), F32)
    fr[0, ctx] = slab[...]

    barrier = pltpu.get_barrier_semaphore()
    greeted = 0
    for p in (pipe, prev, follow):
        for o in range(nctx):
            if p is pipe and o == 0:
                continue
            pl.semaphore_signal(barrier, inc=1, device_id=dev(p, ctx_at(o), dp), device_id_type=MESH)
            greeted += 1
    for o in range(1, ndp):
        pl.semaphore_signal(barrier, inc=1, device_id=dev(pipe, ctx, dp_at(o)), device_id_type=MESH)
        greeted += 1
    pl.semaphore_wait(barrier, greeted)

    up_z = lax.max(ctx - 1, 0)
    down_z = lax.min(ctx + 1, nctx - 1)
    head, tail = pl.ds(0, halo), pl.ds(nrow - halo, halo)
    to_bot = remote(hid.at[0, head, :], hbot, halo_send.at[0], halo_recv.at[0], dev(pipe, up_z, dp))
    to_top = remote(hid.at[0, tail, :], htop, halo_send.at[1], halo_recv.at[1], dev(pipe, down_z, dp))
    to_cbot = remote(cot.at[0, head, :], cbot, halo_send.at[2], halo_recv.at[2], dev(prev, up_z, dp))
    to_cot = remote(cot.at[0], cbuf, halo_send.at[3], halo_recv.at[3], dev(prev, ctx, dp))
    has_up, has_down = ctx > 0, ctx < nctx - 1

    @pl.when(has_up)
    def _():
        to_bot.start()

    @pl.when(has_down)
    def _():
        to_top.start()

    own_sends = []
    for o in range(1, nctx):
        own_sends.append(
            remote(slab, fr.at[0, ctx], f_send.at[0, o], f_recv.at[0, ctx], dev(pipe, ctx_at(o), dp))
        )
    for o in range(nctx):
        own_sends.append(
            remote(slab, fr.at[1, ctx], f_send.at[1, o], f_recv.at[1, ctx], dev(prev, ctx_at(o), dp))
        )
    for c in own_sends:
        c.start()

    @pl.when(has_up)
    def _():
        to_cbot.start()

    to_cot.start()

    lane = lax.broadcasted_iota(jnp.int32, (SUB, LANES), 1)

    def spread(dst, first, block):
        for half in range(2):
            piece = block[half * SUB : (half + 1) * SUB, :]
            start = (first + half * SUB) * nb
            for j in range(nb):
                dst[pl.ds(start + j, SUB, stride=nb), :] = piece[:, j * LANES : (j + 1) * LANES]

    def squares(stat, first, block):
        for half in range(2):
            acc = None
            for j in range(nb):
                piece = block[half * SUB : (half + 1) * SUB, j * LANES : (j + 1) * LANES]
                acc = piece * piece if acc is None else acc + piece * piece
            value = jnp.sum(acc, axis=1, keepdims=True)
            stat = jnp.where(lane == first // SUB + half, value, stat)
        return stat

    load_hid.wait()

    def take_hidden(i, stat):
        block = hbuf[pl.ds(pl.multiple_of(i * 16, 16), 16), :].astype(F32)
        spread(xs, halo + i * 16, block)
        return squares(stat, halo + i * 16, block)

    stat = lax.fori_loop(0, nrow // 16, take_hidden, jnp.zeros((SUB, LANES), F32))

    @pl.when(has_down)
    def _():
        remote(hbot, hbot, halo_send.at[0], halo_recv.at[0], dev(pipe, down_z, dp)).wait_recv()

    @pl.when(jnp.logical_not(has_down))
    def _():
        hbot[...] = jnp.zeros(hbot.shape, BF16)

    @pl.when(has_up)
    def _():
        remote(htop, htop, halo_send.at[1], halo_recv.at[1], dev(pipe, up_z, dp)).wait_recv()

    @pl.when(jnp.logical_not(has_up))
    def _():
        htop[...] = jnp.zeros(htop.shape, BF16)

    for first, ref in ((0, htop), (halo + nrow, hbot)):
        block = ref[...].astype(F32)
        spread(xs, first, block)
        stat = squares(stat, first, block)

    def send_stat(stage, value):
        st_send[stage] = value
        st_recv[stage, dp] = value
        for o in range(1, ndp):
            remote(
                st_send.at[stage], st_recv.at[stage, dp], s_send.at[stage, o], s_recv.at[stage, dp],
                dev(pipe, ctx, dp_at(o)),
            ).start()

    def get_stat(stage):
        for o in range(1, ndp):
            there = dp_at(o)
            remote(
                st_send.at[stage], st_recv.at[stage, there], s_send.at[stage, o], s_recv.at[stage, there],
                dev(pipe, ctx, there),
            ).wait()
        value = st_recv[stage, 0]
        for d in range(1, ndp):
            value = value + st_recv[stage, d]
        return value

    def unpack(stage, value, fn):
        for i in range(nstat):
            column = jnp.sum(jnp.where(lane == i, value, 0.0), axis=1, keepdims=True)
            rows[stage, i * SUB : (i + 1) * SUB, :] = jnp.broadcast_to(fn(column), (SUB, LANES))

    def collect(lo, hi):
        def step(i, stat):
            acc = None
            for g in range(groups):
                base = (g * total + i * SUB) * SUB
                for k in range(SUB):
                    piece = parts[pl.ds(base + k, SUB, stride=SUB), :]
                    acc = piece if acc is None else acc + piece
            return jnp.where(lane == i, jnp.sum(acc, axis=1, keepdims=True), stat)

        return lax.fori_loop(lo, hi, step, jnp.zeros((SUB, LANES), F32), unroll=6)

    def build_filters(b):
        for z in range(nctx):
            for k in range(ntap):
                filt[b, k * nb + z * cb : k * nb + (z + 1) * cb, :] = fr[b, z, k * cb : (k + 1) * cb, :]

    def row_scale(value):
        return lax.rsqrt(value / width + EPS)

    send_stat(0, stat)
    for o in range(1, nctx):
        there = ctx_at(o)
        remote(slab, fr.at[0, there], f_send.at[0, o], f_recv.at[0, there], dev(pipe, there, dp)).wait_recv()
    build_filters(0)
    unpack(0, get_stat(0), row_scale)

    def at(w, g):
        return pl.ds(pl.multiple_of(w * nb + g * SUB, SUB), SUB)

    def row_of(stage, w):
        return jnp.broadcast_to(rows[stage, pl.ds(w, 1), :], (SUB, LANES))

    def tap(b, k, g):
        return filt[b, pl.ds(pl.multiple_of(k * nb + g * SUB, SUB), SUB), :]

    def forward(b, lo, unroll):
        def group(g, _):
            fl = [tap(b, k, g) for k in range(ntap)]
            gain, short, long = fl[0], fl[1 : 1 + nshort], fl[1 + nshort :]

            def step(it, carry):
                lag = list(carry[: taps - 1])
                past = list(carry[taps - 1 :])
                for u in range(unroll):
                    w = lo + it * unroll + u
                    x = (xs if b == 0 else ys)[at(w, g), :]
                    xh = x * row_of(b, w)
                    seq = [xh * gain] + lag
                    streams = []
                    for j in range(3):
                        value = short[taps * j] * seq[0]
                        for i in range(1, taps):
                            value = value + short[taps * j + i] * seq[i]
                        streams.append(value)
                    products = [streams[1] * streams[2]] + past
                    mix = long[0] * products[0]
                    for i in range(1, nlong):
                        mix = mix + long[i] * products[i]
                    for n, value in enumerate((xh, streams[0], streams[1], streams[2], mix)):
                        saved[b, n, at(w, g), :] = value
                    if b == 0:
                        inner = (x + streams[0] * mix).astype(BF16).astype(F32)
                        ys[at(w, g), :] = inner
                        spot = pl.multiple_of((g * total + w) * SUB, SUB)
                        parts[pl.ds(spot, SUB), :] = inner * inner
                    lag, past = seq[:-1], products[:-1]
                return tuple(lag + past)

            zero = blank[...]
            lax.fori_loop(0, (total - lo) // unroll, step, (zero,) * (taps - 1 + nlong - 1))
            return 0

        lax.fori_loop(0, groups, group, 0)

    forward(0, 0, 8)
    send_stat(1, collect(0, nstat))

    for z in range(nctx):
        remote(slab, fr.at[1, z], f_send.at[1, z], f_recv.at[1, z], dev(follow, z, dp)).wait_recv()
    build_filters(1)
    unpack(1, get_stat(1), row_scale)
    forward(1, halo // 2, 8)

    remote(cbuf, cbuf, halo_send.at[3], halo_recv.at[3], dev(follow, ctx, dp)).wait_recv()

    @pl.when(has_down)
    def _():
        remote(cbot, cbot, halo_send.at[2], halo_recv.at[2], dev(follow, down_z, dp)).wait_recv()

    @pl.when(jnp.logical_not(has_down))
    def _():
        cbot[...] = jnp.zeros(cbot.shape, BF16)

    def take_cot(i, _):
        spread(zs, halo + i * 16, cbuf[pl.ds(pl.multiple_of(i * 16, 16), 16), :].astype(F32))
        return 0

    lax.fori_loop(0, nrow // 16, take_cot, 0)
    spread(zs, halo + nrow, cbot[...].astype(F32))

    def backward(b, top, unroll):
        def group(g, _):
            fl = [tap(b, k, g) for k in range(ntap)]
            gain, short, long = fl[0], fl[1 : 1 + nshort], fl[1 + nshort :]

            def one(w, state, acc):
                dmix_next, ds_next = state
                here = at(w, g)
                up = zs[here, :]
                if b == 0:
                    up = up + row_of(1, w) * (wd_outer[here, :] - saved[1, 0, here, :] * row_of(2, w))
                    xs[here, :] = up
                xh, query, key, value, mix = [saved[b, n, here, :] for n in range(5)]
                dmix = [up * query] + dmix_next
                dprod = long[0] * dmix[0]
                for i in range(1, nlong):
                    dprod = dprod + long[i] * dmix[i]
                ds = [[up * mix] + ds_next[0], [dprod * value] + ds_next[1], [dprod * key] + ds_next[2]]
                dn = None
                for j in range(3):
                    for i in range(taps):
                        term = short[taps * j + i] * ds[j][i]
                        dn = term if dn is None else dn + term
                weighted = gain * dn
                (wd_outer if b == 1 else wd_inner)[here, :] = weighted
                spot = pl.multiple_of((g * total + w) * SUB, SUB)
                parts[pl.ds(spot, SUB), :] = xh * weighted
                if acc is not None:
                    product, normed = key * value, xh * gain
                    fresh = [acc[0] + xh * dn]
                    for j in range(3):
                        for i in range(taps):
                            fresh.append(acc[1 + taps * j + i] + normed * ds[j][i])
                    for i in range(nlong):
                        fresh.append(acc[1 + nshort + i] + product * dmix[i])
                    acc = fresh
                return (dmix[:-1], [d[:-1] for d in ds]), acc

            def flat(state):
                return tuple(state[0]) + tuple(v for d in state[1] for v in d)

            def unflat(vals):
                n = nlong - 1
                rest = vals[n:]
                m = taps - 1
                return list(vals[:n]), [list(rest[j * m : (j + 1) * m]) for j in range(3)]

            nstate = nlong - 1 + 3 * (taps - 1)

            def warm(it, carry):
                state = unflat(carry)
                for u in range(unroll):
                    state, _ = one(top - 1 - it * unroll - u, state, None)
                return flat(state)

            def main(it, carry):
                state, acc = unflat(carry[:nstate]), list(carry[nstate:])
                for u in range(unroll):
                    state, acc = one(halo + nrow - 1 - it * unroll - u, state, acc)
                return flat(state) + tuple(acc)

            zero = blank[...]
            carry = lax.fori_loop(0, (top - halo - nrow) // unroll, warm, (zero,) * nstate)
            carry = lax.fori_loop(0, nrow // unroll, main, carry + (zero,) * ntap)
            for k in range(ntap):
                grads[pl.ds(pl.multiple_of(k * nb + g * SUB, SUB), SUB), :] = carry[nstate + k]
            return 0

        lax.fori_loop(0, groups, group, 0)

    def split_grads(b):
        for z in range(nctx):
            for k in range(ntap):
                gs[b, z, k * cb : (k + 1) * cb, :] = grads[k * nb + z * cb : k * nb + (z + 1) * cb, :]

    def mean_of(value):
        return value / width

    backward(1, total, 8)
    send_stat(2, collect(halo // SUB, nstat))
    split_grads(1)
    grad_sends = []
    for o in range(nctx):
        z = ctx_at(o)
        grad_sends.append(
            remote(gs.at[1, z], rg.at[1, ctx], g_send.at[1, o], g_recv.at[1, ctx], dev(follow, z, dp))
        )
        grad_sends[-1].start()
    unpack(2, get_stat(2), mean_of)

    backward(0, halo + nrow + halo // 2, 8)
    send_stat(3, collect(halo // SUB, (halo + nrow) // SUB))
    split_grads(0)
    for o in range(1, nctx):
        z = ctx_at(o)
        grad_sends.append(
            remote(gs.at[0, z], rg.at[0, ctx], g_send.at[0, o], g_recv.at[0, ctx], dev(pipe, z, dp))
        )
        grad_sends[-1].start()
    rg[0, ctx] = gs[0, ctx]
    unpack(3, get_stat(3), mean_of)

    def finish(i, _):
        w = halo + i * 16
        halves = [pl.multiple_of(w + half * SUB, SUB) for half in range(2)]
        scales = [rows[0, pl.ds(h, SUB), :] for h in halves]
        means = [rows[3, pl.ds(h, SUB), :] for h in halves]
        for j in range(nb):
            pieces = []
            for half in range(2):
                here = pl.ds(halves[half] * nb + j, SUB, stride=nb)
                pieces.append(xs[here, :] + scales[half] * (wd_inner[here, :] - saved[0, 0, here, :] * means[half]))
            out[0, pl.ds(pl.multiple_of(i * 16, 16), 16), j * LANES : (j + 1) * LANES] = jnp.concatenate(
                pieces, axis=0
            ).astype(BF16)
        return 0

    lax.fori_loop(0, nrow // 16, finish, 0)

    for z in range(nctx):
        remote(gs.at[1, z], rg.at[1, z], g_send.at[1, z], g_recv.at[1, z], dev(prev, z, dp)).wait_recv()
    for o in range(1, nctx):
        z = ctx_at(o)
        remote(gs.at[0, z], rg.at[0, z], g_send.at[0, o], g_recv.at[0, z], dev(pipe, z, dp)).wait_recv()
    result = rg[0, 0] + rg[1, 0]
    for z in range(1, nctx):
        result = result + (rg[0, z] + rg[1, z])
    for k in range(ntap):
        for j in range(cb):
            cols = pl.ds(j * LANES, LANES)
            piece = result[k * cb + j : k * cb + j + 1, :]
            if k == 0:
                gain_out[0:1, cols] = piece
            elif k <= nshort:
                short_out[k - 1, 0:1, cols] = piece
            else:
                long_out[k - 1 - nshort, 0:1, cols] = piece

    @pl.when(has_up)
    def _():
        to_bot.wait_send()
        to_cbot.wait_send()

    @pl.when(has_down)
    def _():
        to_top.wait_send()

    to_cot.wait_send()
    for c in own_sends + grad_sends:
        c.wait_send()


def handed_on(a0, a1, a2, a3, b0, b1, b2, b3):
    b0[...] = a0[...]

    @pl.when(pl.program_id(0) == 0)
    def _():
        b1[...] = a1[...]
        b2[...] = a2[...]
        b3[...] = a3[...]


def swap(values):
    return jnp.transpose(values, (1, 0, 2))


def per_device(mesh, hidden, cotangent, gain_rows, short_taps, long_taps):
    npipe, nctx, ndp = mesh.shape["pipe"], mesh.shape["ctx"], mesh.shape["dp"]
    nrow, chans = hidden.shape[1], hidden.shape[2]
    own = gain_rows.shape[1]
    wide = -(-own // LANES) * LANES
    nshort, nlong = short_taps.shape[1], long_taps.shape[1]
    ntap = 1 + nshort + nlong
    cb = wide // LANES
    nb = nctx * cb
    halo = 2 * (nshort // 3 + nlong - 2)
    total = nrow + 2 * halo
    slab_rows = -(-ntap * cb // SUB) * SUB

    def widen(values):
        if wide == own:
            return values
        lead = values.shape[:-1]
        blocks = values.reshape(lead + (-1, own))
        blocks = jnp.pad(blocks, [(0, 0)] * (len(lead) + 1) + [(0, wide - own)])
        return blocks.reshape(lead + (-1,))

    def narrow(values):
        if wide == own:
            return values
        lead = values.shape[:-1]
        return values.reshape(lead + (-1, wide))[..., :own].reshape(lead + (-1,))

    cfg = dict(
        npipe=npipe, nctx=nctx, ndp=ndp, nrow=nrow, nb=nb, cb=cb, ntap=ntap, nshort=nshort,
        width=float(chans * ndp), halo=halo,
    )
    full = nb * LANES
    dma = pltpu.SemaphoreType.DMA
    vmem = pl.BlockSpec(memory_space=pltpu.VMEM)
    anywhere = pl.BlockSpec(memory_space=pl.ANY)
    shapes = (
        jax.ShapeDtypeStruct((1, nrow, full), BF16),
        jax.ShapeDtypeStruct((1, wide), F32),
        jax.ShapeDtypeStruct((nshort, 1, wide), F32),
        jax.ShapeDtypeStruct((nlong, 1, wide), F32),
    )
    outs = pl.pallas_call(
        functools.partial(kernel, cfg),
        out_shape=shapes,
        in_specs=[anywhere, anywhere, vmem, vmem, vmem],
        out_specs=(vmem, vmem, vmem, vmem),
        scratch_shapes=[
            pltpu.VMEM((nrow, full), BF16),
            pltpu.VMEM((halo, full), BF16),
            pltpu.VMEM((halo, full), BF16),
            pltpu.VMEM((nrow, full), BF16),
            pltpu.VMEM((halo, full), BF16),
            pltpu.VMEM((slab_rows, LANES), F32),
            pltpu.VMEM((2, nctx, slab_rows, LANES), F32),
            pltpu.VMEM((2, ntap * nb, LANES), F32),
            pltpu.VMEM((ntap * nb, LANES), F32),
            pltpu.VMEM((2, nctx, slab_rows, LANES), F32),
            pltpu.VMEM((2, nctx, slab_rows, LANES), F32),
            pltpu.VMEM((total * nb, LANES), F32),
            pltpu.VMEM((total * nb, LANES), F32),
            pltpu.VMEM((total * nb, LANES), F32),
            pltpu.VMEM((total * nb, LANES), F32),
            pltpu.VMEM((total * nb, LANES), F32),
            pltpu.VMEM((2, 5, total * nb, LANES), F32),
            pltpu.VMEM((total * nb, LANES), F32),
            pltpu.VMEM((4, SUB, LANES), F32),
            pltpu.VMEM((4, ndp, SUB, LANES), F32),
            pltpu.VMEM((4, total, LANES), F32),
            pltpu.VMEM((SUB, LANES), F32),
            dma((1,)),
            dma((4,)),
            dma((4,)),
            dma((2, nctx)),
            dma((2, nctx)),
            dma((2, nctx)),
            dma((2, nctx)),
            dma((4, ndp)),
            dma((4, ndp)),
        ],
        compiler_params=pltpu.CompilerParams(
            collective_id=0, has_side_effects=True, vmem_limit_bytes=56 * 1024 * 1024
        ),
        name="relay",
    )(widen(hidden), widen(cotangent), widen(gain_rows), swap(widen(short_taps)), swap(widen(long_taps)))
    passed = [pl.BlockSpec((1, nrow // 2, full), lambda i: (0, i, 0))] + [
        pl.BlockSpec(o.shape, functools.partial(lambda rank, i: (0,) * rank, len(o.shape))) for o in shapes[1:]
    ]
    outs = pl.pallas_call(
        handed_on,
        out_shape=shapes,
        grid=(2,),
        in_specs=passed,
        out_specs=tuple(passed),
        name="handed_on",
    )(*outs)
    return tuple(narrow(o) for o in (outs[0], outs[1], swap(outs[2]), swap(outs[3])))


def solution(mesh):
    in_specs = (
        P("pipe", "ctx", "dp"),
        P("pipe", "ctx", "dp"),
        P("pipe", ("dp", "ctx")),
        P("pipe", None, ("dp", "ctx")),
        P("pipe", None, ("dp", "ctx")),
    )
    out_specs = (
        P("pipe", "ctx", "dp"),
        P("pipe", ("dp", "ctx")),
        P("pipe", None, ("dp", "ctx")),
        P("pipe", None, ("dp", "ctx")),
    )
    return jax.shard_map(
        functools.partial(per_device, mesh), mesh=mesh, in_specs=in_specs, out_specs=out_specs, check_vma=False
    )
```
